32 devices in a mesh: dp: 16 (over z, x, core), tensor: 2 (over y).
Axes of the slice: x: 2, y: 2, z: 4, core: 2. Of those that a mesh axis runs over, the one named last changes fastest.
Arguments:
- resid_in: float32 [16, 256, 768], P('dp', 'tensor'), may hold values from -27 to 27
- encoded: bfloat16 [16, 256, 768], P('dp', 'tensor'), may hold values from -6 to 6
- dec_segments: int32 [16, 256], P('dp'), may hold values from 0 to 3, never falling along the last dimension, each value on 1 to 128 neighbouring positions
- enc_segments: int32 [16, 256], P('dp'), may hold values from 0 to 3, never falling along the last dimension, each value on 1 to 128 neighbouring positions
- out_grad: float32 [16, 256, 768], P('dp', 'tensor'), may hold values from -6 to 6
- gains: float32 [1, 3, 768], P(None, None, ('dp', 'tensor')), may hold values from 0.1 to 1.9
- bias_table: float32 [32, 12], P(None, 'tensor'), may hold values from -4 to 324
- self_query: bfloat16 [1, 768, 768], P(None, 'dp', 'tensor'), may hold values from -0.0546875 to 0.0546875
- self_key: bfloat16 [1, 768, 768], P(None, 'dp', 'tensor'), may hold values from -0.21875 to 0.21875
- self_value: bfloat16 [1, 768, 768], P(None, 'dp', 'tensor'), may hold values from -0.21875 to 0.21875
- self_out: bfloat16 [1, 768, 768], P(None, 'dp', 'tensor'), may hold values from -1.25 to 1.25
- cross_query: bfloat16 [1, 768, 768], P(None, 'dp', 'tensor'), may hold values from -0.0546875 to 0.0546875
- cross_key: bfloat16 [1, 768, 768], P(None, 'dp', 'tensor'), may hold values from -0.21875 to 0.21875
- cross_value: bfloat16 [1, 768, 768], P(None, 'dp', 'tensor'), may hold values from -0.21875 to 0.21875
- cross_out: bfloat16 [1, 768, 768], P(None, 'dp', 'tensor'), may hold values from -1.75 to 1.75
- ff_gate: bfloat16 [1, 768, 2048], P(None, 'dp', 'tensor'), may hold values from -0.21875 to 0.21875
- ff_up: bfloat16 [1, 768, 2048], P(None, 'dp', 'tensor'), may hold values from -0.21875 to 0.21875
- ff_down: bfloat16 [1, 768, 2048], P(None, 'dp', 'tensor'), may hold values from -0.25 to 0.25
Outputs:
- resid_out: float32 [16, 256, 768], P('dp', 'tensor')
- input_gradient: float32 [16, 256, 768], P('dp', 'tensor')
- encoder_gradient: float32 [16, 256, 768], P('dp', 'tensor')
- gains_gradient: float32 [1, 3, 768], P(None, None, ('dp', 'tensor'))
- bias_table_gradient: float32 [32, 12], P(None, 'tensor')
- self_query_gradient: float32 [1, 768, 768], P(None, 'dp', 'tensor')
- self_key_gradient: float32 [1, 768, 768], P(None, 'dp', 'tensor')
- self_value_gradient: float32 [1, 768, 768], P(None, 'dp', 'tensor')
- self_out_gradient: float32 [1, 768, 768], P(None, 'dp', 'tensor')
- cross_query_gradient: float32 [1, 768, 768], P(None, 'dp', 'tensor')
- cross_key_gradient: float32 [1, 768, 768], P(None, 'dp', 'tensor')
- cross_value_gradient: float32 [1, 768, 768], P(None, 'dp', 'tensor')
- cross_out_gradient: float32 [1, 768, 768], P(None, 'dp', 'tensor')
- ff_gate_gradient: float32 [1, 768, 2048], P(None, 'dp', 'tensor')
- ff_up_gradient: float32 [1, 768, 2048], P(None, 'dp', 'tensor')
- ff_down_gradient: float32 [1, 768, 2048], P(None, 'dp', 'tensor')
The draws below stay inside these ranges and needn't reach their ends.
Inputs may be any that keep to these rules, and one draw needn't show every extreme that they name: `dec_segments`: in every sequence the numbers never fall, each of 0 to 3 occurs, and a document has at most 128 tokens. `enc_segments`: in every sequence the numbers never fall, each of 0 to 3 occurs, and a document has at most 128 tokens.
All inputs are finite; a program needn't handle non-finite values.
Results may differ from the reference program's by a relative error of at most 0.035.
Values may be sent and summed in bfloat16 or wider, within the bound.
No kernel may reach another device: no remote copies, remote signals or barrier semaphores. Data moves between devices by JAX's collectives and lax.ppermute only.
A program may use at most 128 MiB of HBM per device.

```python
import math
import jax
import jax.numpy as jnp
import numpy as np
from jax import lax

D = 768
HEADS = 12
HEAD_DIM = 64
FF = 2048
BUCKETS = 32
LAYERS = 1
LEN = 256
ENC_LEN = 256
DOCS = 4
INNER = 768
SEQS = 16


def draw_resid_in(key, part):
    base_key, row_key, col_key = jax.random.split(jax.random.fold_in(key, 11), 3)
    shape = (SEQS, LEN, D)
    base = jnp.clip(jax.random.normal(base_key, shape, jnp.float32), -4.0, 4.0)
    row_scale = jnp.exp(jax.random.uniform(row_key, (SEQS, LEN, 1), jnp.float32, math.log(0.3), math.log(3.0)))
    col_scale = jnp.exp(jax.random.uniform(col_key, (1, 1, D), jnp.float32, math.log(0.7), math.log(1.5)))
    rising = 0.5 + lax.broadcasted_iota(jnp.float32, (SEQS, 1, 1), 0) / max(SEQS - 1, 1)
    return base * row_scale * col_scale * rising


def draw_bias_table(key, part):
    base_key = jax.random.fold_in(jax.random.fold_in(key, 23), 0)
    base = jnp.clip(jax.random.normal(base_key, (BUCKETS, HEADS), jnp.float32), -4.0, 4.0)
    return base


def spiked(entries, own_key, source, target, shards_of, factor):
    def block_of(position):
        return (jnp.arange(entries.shape[position]) // (entries.shape[position] // shards_of)).reshape((-1,) + (1,) * (entries.ndim - 1 - position))

    one_side = jax.random.permutation(own_key, shards_of)[block_of(target)]
    far = (block_of(target) + shards_of // 2) % shards_of
    return jnp.where((block_of(source) == one_side) | (block_of(source) == far), factor * entries, entries)


def shard_levels(rng, extent, pieces, least, top_value):
    level, own = 1.0, jax.random.fold_in(rng, 6)
    for position, parts in pieces:
        heights = jnp.exp(jax.random.uniform(jax.random.fold_in(own, position), (parts,), jnp.float32, least / len(pieces), top_value / len(pieces)))
        level = level * jnp.repeat(heights, extent[position] // parts).reshape([-1 if axis == position else 1 for axis in range(len(extent))])
    return level


def split_up(count, total, limit, lean):
    portions = [(1 << 20) // math.isqrt(rank ** lean) + 1 for rank in range(2, count + 1)]
    surplus, counts = total - limit - (count - 1), [1] * (count - 1)
    while surplus > 0:
        free = [i for i in range(count - 1) if counts[i] < limit]
        whole, budget = sum([portions[i] for i in free]), surplus
        for i in free:
            more = min(limit - counts[i], max(1, budget * portions[i] // whole), surplus)
            counts[i] = counts[i] + more
            surplus = surplus - more
    return np.array([limit] + counts)


def uneven(key, count, total, most, slope):
    if count == 2:
        one = jax.random.randint(key, (), max(1, total - most), min(most, total - 1) + 1)
        return jnp.stack([one, total - one])
    sizes = jnp.asarray(split_up(count, total, most, slope), jnp.int32)
    twos = (count - 1) // 2
    giver, taker = sizes[1:1 + 2 * twos:2], sizes[2:2 + 2 * twos:2]
    slack = jnp.minimum(giver - 1, most - taker)
    passed = jax.random.randint(jax.random.fold_in(key, 1), (twos,), 0, 1 << 20) % (slack + 1)
    sizes = sizes.at[1:1 + 2 * twos:2].set(giver - passed).at[2:2 + 2 * twos:2].set(taker + passed)
    return sizes[jax.random.permutation(jax.random.fold_in(key, 2), count)]


def noise(stream_key, extent, spread, most, cuts=(), kind=jnp.bfloat16):
    values = jax.random.normal(stream_key, extent, jnp.float32) * spread
    if len(cuts) > 0:
        values = shard_levels(stream_key, extent, cuts, -0.22, 0.18) * values
    return jnp.clip(values, min=-most, max=most).astype(kind)


def bell_draw_with(stream_key, extent, spread, limit, pieces, heavy, held_as=jnp.bfloat16):
    entries = spread * jax.random.normal(stream_key, extent, jnp.float32)
    if pieces:
        entries = entries * shard_levels(stream_key, extent, pieces, -0.22, 0.18)
    return jnp.clip(spiked(entries, jax.random.fold_in(stream_key, 3), *heavy), -limit, limit).astype(held_as)


def setup_inputs(seed: int = 0) -> dict:
    key_list = jax.random.split(jax.random.key(seed), 19)
    return {
        "resid_in": draw_resid_in(jax.random.fold_in(key_list[18], 71), 0),
        "encoded": noise(key_list[1], (SEQS, ENC_LEN, D), 1.0, 6.0, ((0, 16), (1, 2))),
        "dec_segments": jax.vmap(lambda own: jnp.searchsorted(jnp.cumsum(uneven(own, DOCS, LEN, LEN // 2, 1)), jnp.arange(LEN), side="right"))(jax.random.split(key_list[2], SEQS)).reshape((SEQS, LEN)).astype(jnp.int32),
        "enc_segments": jax.vmap(lambda own: jnp.searchsorted(jnp.cumsum(uneven(own, DOCS, ENC_LEN, ENC_LEN // 2, 1)), jnp.arange(ENC_LEN), side="right"))(jax.random.split(key_list[3], SEQS)).reshape((SEQS, ENC_LEN)).astype(jnp.int32),
        "out_grad": bell_draw_with(key_list[4], (SEQS, LEN, D), 1.0, 6.0, ((0, 16), (1, 2)), (0, 2, 16, 2.0), jnp.float32),
        "gains": jnp.clip(1.0 + 0.18 * jax.random.normal(key_list[5], (LAYERS, 3, D), jnp.float32), 0.1, 1.9),
        "bias_table": draw_bias_table(jax.random.fold_in(key_list[18], 71), 0),
        "self_query": noise(key_list[7], (LAYERS, D, INNER), (D * 16) ** -0.5, 0.0546875, ((1, 16), (2, 2))),
        "self_key": noise(key_list[8], (LAYERS, D, INNER), D ** -0.5, 0.21875, ((1, 16), (2, 2))),
        "self_value": noise(key_list[9], (LAYERS, D, INNER), D ** -0.5, 0.21875, ((1, 16), (2, 2))),
        "self_out": noise(key_list[10], (LAYERS, D, INNER), (D // 32) ** -0.5, 1.25, ((1, 16), (2, 2))),
        "cross_query": noise(key_list[11], (LAYERS, D, INNER), (D * 16) ** -0.5, 0.0546875, ((1, 16), (2, 2))),
        "cross_key": noise(key_list[12], (LAYERS, D, INNER), D ** -0.5, 0.21875, ((1, 16), (2, 2))),
        "cross_value": noise(key_list[13], (LAYERS, D, INNER), D ** -0.5, 0.21875, ((1, 16), (2, 2))),
        "cross_out": noise(key_list[14], (LAYERS, D, INNER), (D // 64) ** -0.5, 1.75, ((1, 16), (2, 2))),
        "ff_gate": noise(key_list[15], (LAYERS, D, FF), D ** -0.5, 0.21875, ((1, 16), (2, 2))),
        "ff_up": noise(key_list[16], (LAYERS, D, FF), D ** -0.5, 0.21875, ((1, 16), (2, 2))),
        "ff_down": noise(key_list[17], (LAYERS, D, FF), (FF // 4) ** -0.5, 0.25, ((1, 16), (2, 2))),
    }


epsilon = 1e-06
bucket_steps = [math.ceil(16 * 8 ** (step / 16)) for step in range(1, 16)]

def rounded(value_heads):
    return lax.optimization_barrier(value_heads.astype(jnp.bfloat16))

def widened(value_heads):
    return value_heads.astype(jnp.float32)

def matmul(left, right):
    return jnp.dot(left, right, preferred_element_type=jnp.float32)

def norm_rows(residual_stream, gain):
    inverse = lax.rsqrt(lax.optimization_barrier(jnp.mean(residual_stream * residual_stream, axis=-1, keepdims=True)) + epsilon)
    return residual_stream * inverse * gain

def gelu_tanh(value_heads):
    return jax.nn.gelu(value_heads, approximate=True)

def bucket_index(length):
    rows = lax.broadcasted_iota(jnp.int32, (length, length), 0)
    columns = lax.broadcasted_iota(jnp.int32, (length, length), 1)
    distance = jnp.maximum(rows - columns, 0)
    beyond = jnp.full((length, length), 16, jnp.int32)
    for edge in bucket_steps:
        beyond = beyond + (distance >= edge).astype(jnp.int32)
    return jnp.where(distance < 16, distance, beyond)

def divide_heads(matrix):
    return matrix.reshape(matrix.shape[0], HEADS, HEAD_DIM)

def merge_heads(matrix):
    return matrix.reshape(matrix.shape[0], INNER)

def masked_scores(query_heads, key_heads, extra, allowed):
    scores = jnp.einsum('ihd,jhd->hij', widened(query_heads), widened(key_heads)) + extra
    return jnp.where(allowed, scores, -jnp.inf)

def attend(query_heads, key_heads, value_heads, extra, allowed):
    scores = masked_scores(query_heads, key_heads, extra, allowed)
    top = lax.optimization_barrier(jnp.max(scores, axis=-1, keepdims=True))
    raised = jnp.exp(scores - top)
    total = lax.optimization_barrier(jnp.sum(raised, axis=-1, keepdims=True))
    shares = rounded(raised / total)
    mixed = rounded(jnp.einsum('hij,jhd->ihd', widened(shares), widened(value_heads)))
    return (mixed, top + jnp.log(total))

def attend_back(query_heads, key_heads, value_heads, extra, allowed, log_total, mixed_heads_gradient):
    shares = jnp.exp(masked_scores(query_heads, key_heads, extra, allowed) - log_total)
    value_heads_gradient = rounded(jnp.einsum('hij,ihd->jhd', widened(rounded(shares)), widened(mixed_heads_gradient)))
    back_shares = jnp.einsum('ihd,jhd->hij', widened(mixed_heads_gradient), widened(value_heads))
    delta = lax.optimization_barrier(jnp.sum(shares * back_shares, axis=-1, keepdims=True))
    back_scores = shares * (back_shares - delta)
    low_scores = widened(rounded(back_scores))
    query_rows_gradient = rounded(jnp.einsum('hij,jhd->ihd', low_scores, widened(key_heads)))
    key_heads_gradient = rounded(jnp.einsum('hij,ihd->jhd', low_scores, widened(query_heads)))
    return (query_rows_gradient, key_heads_gradient, value_heads_gradient, back_scores)

def layer_forward(residual_stream, encoder, gain, weights, bias, allowed_self, allowed_cross):
    query_matrix, key_matrix, value_matrix, output_matrix, cross_query_matrix, cross_key_matrix, cross_value_matrix, cross_output_matrix, gate_matrix, up_projection_matrix, down_projection_matrix = weights
    self_normed_rows = rounded(norm_rows(residual_stream, gain[0]))
    query_heads = divide_heads(rounded(matmul(self_normed_rows, query_matrix)))
    key_heads = divide_heads(rounded(matmul(self_normed_rows, key_matrix)))
    value_heads = divide_heads(rounded(matmul(self_normed_rows, value_matrix)))
    self_mixed_heads, total_a = attend(query_heads, key_heads, value_heads, bias, allowed_self)
    residual_after_self = residual_stream + matmul(merge_heads(self_mixed_heads), output_matrix.T)
    cross_normed_rows = rounded(norm_rows(residual_after_self, gain[1]))
    ask_cross = divide_heads(rounded(matmul(cross_normed_rows, cross_query_matrix)))
    key_cross = divide_heads(rounded(matmul(encoder, cross_key_matrix)))
    value_cross = divide_heads(rounded(matmul(encoder, cross_value_matrix)))
    cross_mixed_heads, total_b = attend(ask_cross, key_cross, value_cross, 0.0, allowed_cross)
    residual_after_cross = residual_after_self + matmul(merge_heads(cross_mixed_heads), cross_output_matrix.T)
    feed_normed_rows = rounded(norm_rows(residual_after_cross, gain[2]))
    gate_branch = matmul(feed_normed_rows, gate_matrix)
    upper_branch = matmul(feed_normed_rows, up_projection_matrix)
    hidden_state = rounded(gelu_tanh(gate_branch) * upper_branch)
    residual_after_feed = residual_after_cross + matmul(hidden_state, down_projection_matrix.T)
    saved = (residual_stream, self_normed_rows, query_heads, key_heads, value_heads, total_a, self_mixed_heads, residual_after_self, cross_normed_rows, ask_cross, key_cross, value_cross, total_b, cross_mixed_heads, residual_after_cross, feed_normed_rows, gate_branch, upper_branch, hidden_state)
    return (residual_after_feed, saved)

def norm_step(upstream, rows, gain, normed_state_gradient):
    unused, norm_back = jax.vjp(norm_rows, rows, gain)
    back_rows, back_gain = norm_back(normed_state_gradient)
    return (upstream + back_rows, back_gain)

def layer_backward(upstream, back_encoder, back_bias, encoder, gain, weights, bias, allowed_self, allowed_cross, saved):
    query_matrix, key_matrix, value_matrix, output_matrix, cross_query_matrix, cross_key_matrix, cross_value_matrix, cross_output_matrix, gate_matrix, up_projection_matrix, down_projection_matrix = weights
    residual_stream, self_normed_rows, query_heads, key_heads, value_heads, total_a, self_mixed_heads, residual_after_self, cross_normed_rows, ask_cross, key_cross, value_cross, total_b, cross_mixed_heads, residual_after_cross, feed_normed_rows, gate_branch, upper_branch, hidden_state = saved
    sent_gradient = rounded(upstream)
    down_matrix_gradient = matmul(sent_gradient.T, hidden_state)
    hidden_state_gradient = matmul(sent_gradient, down_projection_matrix)
    active, gelu_back = jax.vjp(gelu_tanh, gate_branch)
    gate_branch_gradient = rounded(gelu_back(hidden_state_gradient * upper_branch)[0])
    upper_branch_gradient = rounded(hidden_state_gradient * active)
    gate_matrix_gradient = matmul(feed_normed_rows.T, gate_branch_gradient)
    up_matrix_gradient = matmul(feed_normed_rows.T, upper_branch_gradient)
    normed_state_gradient = matmul(gate_branch_gradient, gate_matrix.T) + matmul(upper_branch_gradient, up_projection_matrix.T)
    upstream, gain_c = norm_step(upstream, residual_after_cross, gain[2], normed_state_gradient)
    sent_gradient = rounded(upstream)
    cross_output_matrix_gradient = matmul(sent_gradient.T, merge_heads(cross_mixed_heads))
    mixed_heads_gradient = divide_heads(rounded(matmul(sent_gradient, cross_output_matrix)))
    query_cross_gradient, key_rows_gradient, value_rows_gradient, unused = attend_back(ask_cross, key_cross, value_cross, 0.0, allowed_cross, total_b, mixed_heads_gradient)
    query_cross_gradient = merge_heads(query_cross_gradient)
    key_rows_gradient = merge_heads(key_rows_gradient)
    value_rows_gradient = merge_heads(value_rows_gradient)
    cross_query_matrix_gradient = matmul(cross_normed_rows.T, query_cross_gradient)
    cross_key_matrix_gradient = matmul(encoder.T, key_rows_gradient)
    cross_value_matrix_gradient = matmul(encoder.T, value_rows_gradient)
    back_encoder = back_encoder + matmul(key_rows_gradient, cross_key_matrix.T) + matmul(value_rows_gradient, cross_value_matrix.T)
    upstream, gain_b = norm_step(upstream, residual_after_self, gain[1], matmul(query_cross_gradient, cross_query_matrix.T))
    sent_gradient = rounded(upstream)
    output_matrix_gradient = matmul(sent_gradient.T, merge_heads(self_mixed_heads))
    mixed_heads_gradient = divide_heads(rounded(matmul(sent_gradient, output_matrix)))
    query_rows_gradient, key_heads_gradient, value_heads_gradient, back_scores = attend_back(query_heads, key_heads, value_heads, bias, allowed_self, total_a, mixed_heads_gradient)
    back_bias = back_bias + back_scores
    query_rows_gradient = merge_heads(query_rows_gradient)
    key_heads_gradient = merge_heads(key_heads_gradient)
    value_heads_gradient = merge_heads(value_heads_gradient)
    query_matrix_gradient = matmul(self_normed_rows.T, query_rows_gradient)
    key_matrix_gradient = matmul(self_normed_rows.T, key_heads_gradient)
    value_matrix_gradient = matmul(self_normed_rows.T, value_heads_gradient)
    normed_state_gradient = matmul(query_rows_gradient, query_matrix.T) + matmul(key_heads_gradient, key_matrix.T) + matmul(value_heads_gradient, value_matrix.T)
    upstream, gain_a = norm_step(upstream, residual_stream, gain[0], normed_state_gradient)
    gradients = (query_matrix_gradient, key_matrix_gradient, value_matrix_gradient, output_matrix_gradient, cross_query_matrix_gradient, cross_key_matrix_gradient, cross_value_matrix_gradient, cross_output_matrix_gradient, gate_matrix_gradient, up_matrix_gradient, down_matrix_gradient)
    return (upstream, back_encoder, back_bias, gradients, jnp.stack([gain_a, gain_b, gain_c]))

def reference(resid_in, encoded, dec_segments, enc_segments, out_grad, gains, bias_table, self_query, self_key, self_value, self_out, cross_query, cross_key, cross_value, cross_out, ff_gate, ff_up, ff_down):
    matrices = (self_query, self_key, self_value, self_out, cross_query, cross_key, cross_value, cross_out, ff_gate, ff_up, ff_down)
    bucket = bucket_index(LEN)
    bias = jnp.transpose(jnp.take(bias_table, bucket, axis=0), (2, 0, 1))
    causal = lax.broadcasted_iota(jnp.int32, (LEN, LEN), 0) >= lax.broadcasted_iota(jnp.int32, (LEN, LEN), 1)

    def one_sequence(carry, item):
        totals, gain_total, bias_total = carry
        residual_stream, encoder, dec_row, enc_row, upstream = item
        allowed_self = causal & (dec_row[:, None] == dec_row[None, :])
        allowed_cross = dec_row[:, None] == enc_row[None, :]
        stored = []
        for layer in range(LAYERS):
            weights = tuple((matrix[layer] for matrix in matrices))
            residual_stream, saved = layer_forward(residual_stream, encoder, gains[layer], weights, bias, allowed_self, allowed_cross)
            stored.append(saved)
        back_encoder = jnp.zeros((ENC_LEN, D), jnp.float32)
        per_layer = {}
        gain_layers = {}
        for layer in reversed(range(LAYERS)):
            weights = tuple((matrix[layer] for matrix in matrices))
            outcome = layer_backward(upstream, back_encoder, bias_total, encoder, gains[layer], weights, bias, allowed_self, allowed_cross, stored[layer])
            upstream, back_encoder, bias_total = (outcome[0], outcome[1], outcome[2])
            per_layer[layer] = outcome[3]
            gain_layers[layer] = outcome[4]
        totals = tuple((totals[index] + jnp.stack([per_layer[layer][index] for layer in range(LAYERS)]) for index in range(len(matrices))))
        gain_total = gain_total + jnp.stack([gain_layers[layer] for layer in range(LAYERS)])
        return ((totals, gain_total, bias_total), (residual_stream, upstream, back_encoder))
    start = (tuple((jnp.zeros(matrix.shape, jnp.float32) for matrix in matrices)), jnp.zeros((LAYERS, 3, D), jnp.float32), jnp.zeros((HEADS, LEN, LEN), jnp.float32))
    finish, outputs = lax.scan(one_sequence, start, (resid_in, encoded, dec_segments, enc_segments, out_grad))
    totals, gain_total, bias_total = finish
    table_gradient = jax.ops.segment_sum(bias_total.reshape(HEADS, LEN * LEN).T, bucket.reshape(LEN * LEN), num_segments=BUCKETS)
    return (outputs[0], outputs[1], outputs[2], gain_total, table_gradient, totals[0], totals[1], totals[2], totals[3], totals[4], totals[5], totals[6], totals[7], totals[8], totals[9], totals[10])
```

```python
import math

import jax
import jax.numpy as jnp
from jax import lax
from jax.experimental import pallas as pl
from jax.experimental.pallas import tpu as pltpu
from jax.sharding import PartitionSpec as P

HEAD_DIM = 64

epsilon = 1e-06
bucket_steps = [math.ceil(16 * 8 ** (step / 16)) for step in range(1, 16)]


def line_sizes(count):
    tail = [2] if count % 2 == 0 else []
    rest = count // 2 if tail else count
    sizes = []
    while rest > 1:
        step = 4 if rest % 4 == 0 else 2 if rest % 2 == 0 else rest
        sizes.append(step)
        rest //= step
    return sizes + tail


def line_strides(sizes):
    strides = []
    stride = 1
    for size in reversed(sizes):
        strides.insert(0, stride)
        stride *= size
    return strides


def spread_shard(shard, count):
    sizes = line_sizes(count)
    strides = line_strides(sizes)
    pieces = [(shard, list(range(count)))]
    for size, stride in zip(sizes, strides):
        fresh = []
        for piece, origin in pieces:
            if size == 2:
                pairs = [(i, i ^ stride) for i in range(count) if origin[i] >= 0]
                moved = [-1] * count
                for source, target in pairs:
                    moved[target] = origin[source]
                fresh.append((lax.ppermute(piece, "dp", pairs), moved))
                continue
            runs = [(piece, origin, 1), (piece, origin, -1)]
            for hop in range(1, size):
                following = []
                for current, known, way in runs:
                    pairs = [
                        (i, i + way * stride)
                        for i in range(count)
                        if known[i] >= 0 and 0 <= (i // stride) % size + way < size
                    ]
                    moved = [-1] * count
                    for source, target in pairs:
                        moved[target] = known[source]
                    arrived = lax.ppermute(current, "dp", pairs)
                    fresh.append((arrived, moved))
                    following.append((arrived, moved, way))
                runs = following
        pieces = pieces + fresh
    return pieces


def assemble(pieces, count, name):
    arrays = [piece for piece, _ in pieces]
    table = jnp.asarray([origin for _, origin in pieces], jnp.int32)
    places = lax.dynamic_index_in_dim(table, lax.axis_index("dp"), 1, keepdims=False)
    parts, rows, columns = arrays[0].shape
    number = len(arrays)
    aligned = rows % 16 == 0
    whole = (parts, count * rows, columns) if aligned else (parts, count, rows, columns)

    def body(places_ref, *refs):
        sources, out, arrived = refs[:number], refs[number], refs[number + 1]

        def copy(index):
            origin = jnp.maximum(places_ref[index], 0)
            if aligned:
                target = out.at[:, pl.ds(pl.multiple_of(origin * rows, 16), rows), :]
            else:
                target = out.at[:, origin]
            return pltpu.make_async_copy(sources[index], target, arrived.at[index])

        for index in range(number):

            @pl.when(places_ref[index] >= 0)
            def _():
                copy(index).start()

        for index in range(number):

            @pl.when(places_ref[index] >= 0)
            def _():
                copy(index).wait()

    return pl.pallas_call(
        body,
        out_shape=jax.ShapeDtypeStruct(whole, arrays[0].dtype),
        in_specs=[pl.BlockSpec(memory_space=pltpu.SMEM)]
        + [pl.BlockSpec(memory_space=pl.ANY)] * number,
        out_specs=pl.BlockSpec(memory_space=pl.ANY),
        scratch_shapes=[pltpu.SemaphoreType.DMA((number,))],
        name=name,
    )(places, *arrays).reshape(parts, count * rows, columns)


def add_low(*terms):
    total = terms[0].astype(jnp.float32)
    for term in terms[1:]:
        total = total + term.astype(jnp.float32)
    return total


def reduce_blocks(blocks, count):
    sizes = line_sizes(count)
    strides = line_strides(sizes)
    own = lax.axis_index("dp")
    value = blocks.reshape(tuple(sizes) + blocks.shape[1:])
    recv = None
    for dim in reversed(range(len(sizes))):
        size, stride = sizes[dim], strides[dim]
        here = (own // stride) % size

        def block(index):
            chosen = lax.dynamic_index_in_dim(value, index, dim, keepdims=False)
            if recv is None:
                return chosen
            return add_low(chosen, *[lax.dynamic_index_in_dim(r, index, dim, keepdims=False) for r in recv])

        if size == 2:
            pairs = [(i, i ^ stride) for i in range(count)]
            got = [lax.ppermute(block(1 - here).astype(jnp.bfloat16), "dp", pairs)]
        else:
            got = []
            for way in (1, -1):
                carried = None
                for hop in reversed(range(1, size)):
                    target = jnp.clip(here + way * hop, 0, size - 1)
                    outgoing = block(target)
                    if carried is not None:
                        outgoing = add_low(outgoing, carried)
                    pairs = [
                        (i, i + way * stride)
                        for i in range(count)
                        if 0 <= (i // stride) % size + way * hop < size
                    ]
                    carried = lax.ppermute(outgoing.astype(jnp.bfloat16), "dp", pairs)
                got.append(carried)
        value = block(here)
        recv = got
    return add_low(value, *recv)


def butterfly(value, axis, count):
    if count & (count - 1):
        return lax.psum(value, axis)
    step = 1
    while step < count:
        value = value + lax.ppermute(value, axis, [(i, i ^ step) for i in range(count)])
        step *= 2
    return value


def swap_sum(part, count):
    low = part.astype(jnp.bfloat16)
    total = low.astype(jnp.float32)
    for shift in range(1, count):
        total = total + lax.ppermute(
            low, "tensor", [(i, (i + shift) % count) for i in range(count)]
        ).astype(jnp.float32)
    return total


def gather_tokens(rows, count):
    if count != 2:
        return lax.all_gather(rows, "tensor", axis=0, tiled=True)
    other = lax.ppermute(rows, "tensor", [(0, 1), (1, 0)])
    first = lax.axis_index("tensor") == 0
    return jnp.concatenate([jnp.where(first, rows, other), jnp.where(first, other, rows)], axis=0)


def matmul(left, right):
    return jnp.dot(left, right, preferred_element_type=jnp.float32)


def matmul_nt(left, right):
    return lax.dot_general(left, right, (((1,), (1,)), ((), ())), preferred_element_type=jnp.float32)


def matmul_tn(left, right):
    return lax.dot_general(left, right, (((0,), (0,)), ((), ())), preferred_element_type=jnp.float32)


def gated_product(left, right, form):
    return jnp.einsum(form, left, right, preferred_element_type=jnp.float32)


def norm_rows(rows, gain):
    inverse = lax.rsqrt(jnp.mean(rows * rows, axis=-1, keepdims=True) + epsilon)
    return rows * inverse * gain


def norm_step(upstream, rows, gain, gradient):
    unused, norm_back = jax.vjp(norm_rows, rows, gain)
    back_rows, back_gain = norm_back(gradient)
    return (upstream + back_rows, back_gain)


def gelu_tanh(values):
    return jax.nn.gelu(values, approximate=True)


def bucket_of(distance):
    beyond = jnp.full(distance.shape, 16, jnp.int32)
    for edge in bucket_steps:
        beyond = beyond + (distance >= edge).astype(jnp.int32)
    return jnp.where(distance < 16, distance, beyond)


def bucket_index(length):
    rows = lax.broadcasted_iota(jnp.int32, (length, length), 0)
    columns = lax.broadcasted_iota(jnp.int32, (length, length), 1)
    return bucket_of(jnp.maximum(rows - columns, 0))


def table_bias(bucket, table):
    labels = lax.broadcasted_iota(jnp.int32, (1, 1, table.shape[0]), 2)
    indicator = (bucket[:, :, None] == labels).astype(jnp.float32)
    return jnp.einsum("ijb,bh->hij", indicator, table, precision=lax.Precision.HIGHEST)


def table_gradient(bucket, back_bias, buckets):
    labels = lax.broadcasted_iota(jnp.int32, (1, 1, buckets), 2)
    indicator = (bucket[:, :, None] == labels).astype(jnp.float32)
    return jnp.einsum("ijb,hij->bh", indicator, back_bias, precision=lax.Precision.HIGHEST)


def divide_heads(matrix):
    return matrix.reshape(matrix.shape[0], -1, HEAD_DIM)


def merge_heads(matrix):
    return matrix.reshape(matrix.shape[0], -1)


def low(value):
    return value.astype(jnp.bfloat16)


def masked_scores(query, key, extra, allowed):
    return jnp.where(allowed, gated_product(query, key, "ihd,jhd->hij") + extra, -jnp.inf)


def attend(query, key, value, extra, allowed):
    scores = masked_scores(query, key, extra, allowed)
    top = jnp.max(scores, axis=-1, keepdims=True)
    raised = jnp.exp(scores - top)
    total = jnp.sum(raised, axis=-1, keepdims=True)
    mixed = low(gated_product(low(raised / total), value, "hij,jhd->ihd"))
    return (mixed, top + jnp.log(total))


def attend_back(query, key, value, extra, allowed, log_total, back_mixed):
    shares = jnp.exp(masked_scores(query, key, extra, allowed) - log_total)
    back_value = low(gated_product(low(shares), back_mixed, "hij,ihd->jhd"))
    back_shares = gated_product(back_mixed, value, "ihd,jhd->hij")
    delta = jnp.sum(shares * back_shares, axis=-1, keepdims=True)
    back_scores = shares * (back_shares - delta)
    low_scores = low(back_scores)
    back_query = low(gated_product(low_scores, key, "hij,jhd->ihd"))
    back_key = low(gated_product(low_scores, query, "hij,ihd->jhd"))
    return (back_query, back_key, back_value, back_scores)


def per_device(count, pair):
    def run(
        resid_in, encoded, dec_segments, enc_segments, out_grad, gains, bias_table,
        self_query, self_key, self_value, self_out,
        cross_query, cross_key, cross_value, cross_out,
        ff_gate, ff_up, ff_down,
    ):
        tokens_here = resid_in.shape[1]
        length = dec_segments.shape[1]
        half = lax.axis_index("tensor")

        def gathered(matrices, name):
            return assemble(spread_shard(jnp.concatenate(matrices, axis=0), count), count, name)

        width = gains.shape[2]
        place = (lax.axis_index("dp") * pair + half) * width
        gain = lax.dynamic_update_slice(
            jnp.zeros((gains.shape[1], width * count * pair), jnp.float32), gains[0], (0, place)
        )
        gain = butterfly(butterfly(gain, "dp", count), "tensor", pair)

        residual = gather_tokens(resid_in[0], pair)
        encoder = gather_tokens(encoded[0], pair)
        upstream = gather_tokens(out_grad[0], pair)

        self_all = gathered((self_query, self_key, self_value, self_out), "gather_self")
        cross_all = gathered((cross_query, cross_key, cross_value, cross_out), "gather_cross")
        feed_all = gathered((ff_gate, ff_up, ff_down), "gather_feed")
        query_m, key_m, value_m, out_m = (self_all[i] for i in range(4))
        cquery_m, ckey_m, cvalue_m, cout_m = (cross_all[i] for i in range(4))
        gate_m, up_m, down_m = (feed_all[i] for i in range(3))

        bucket = bucket_index(length)
        bias = table_bias(bucket, bias_table)
        causal = lax.broadcasted_iota(jnp.int32, (length, length), 0) >= lax.broadcasted_iota(
            jnp.int32, (length, length), 1
        )
        dec, enc = dec_segments[0], enc_segments[0]
        allowed_self = causal & (dec[:, None] == dec[None, :])
        allowed_cross = dec[:, None] == enc[None, :]

        normed_a = low(norm_rows(residual, gain[0]))
        query = divide_heads(low(matmul(normed_a, query_m)))
        key = divide_heads(low(matmul(normed_a, key_m)))
        value = divide_heads(low(matmul(normed_a, value_m)))
        mixed_a, total_a = attend(query, key, value, bias, allowed_self)
        after_a = residual + swap_sum(matmul_nt(merge_heads(mixed_a), out_m), pair)
        normed_b = low(norm_rows(after_a, gain[1]))
        ask = divide_heads(low(matmul(normed_b, cquery_m)))
        key_cross = divide_heads(low(matmul(encoder, ckey_m)))
        value_cross = divide_heads(low(matmul(encoder, cvalue_m)))
        mixed_b, total_b = attend(ask, key_cross, value_cross, 0.0, allowed_cross)
        after_b = after_a + swap_sum(matmul_nt(merge_heads(mixed_b), cout_m), pair)
        normed_c = low(norm_rows(after_b, gain[2]))
        gate = matmul(normed_c, gate_m)
        upper = matmul(normed_c, up_m)
        active, gelu_back = jax.vjp(gelu_tanh, gate)
        hidden = low(active * upper)

        sent_c = low(upstream)
        back_hidden = matmul(sent_c, down_m)
        back_gate = low(gelu_back(back_hidden * upper)[0])
        back_upper = low(back_hidden * active)
        back_normed = swap_sum(matmul_nt(back_gate, gate_m) + matmul_nt(back_upper, up_m), pair)
        resid_out = after_b + swap_sum(matmul_nt(hidden, down_m), pair)

        def reduced(parts):
            stack = jnp.stack([low(part) for part in parts])
            blocks = stack.reshape(len(parts), count, -1, stack.shape[-1])
            return reduce_blocks(jnp.transpose(blocks, (1, 0, 2, 3)), count)

        feed_sum = reduced(
            (matmul_tn(normed_c, back_gate), matmul_tn(normed_c, back_upper), matmul_tn(sent_c, hidden))
        )
        upstream, gain_c = norm_step(upstream, after_b, gain[2], back_normed)

        sent_b = low(upstream)
        back_mixed = divide_heads(low(matmul(sent_b, cout_m)))
        back_ask, back_key, back_value, unused = attend_back(
            ask, key_cross, value_cross, 0.0, allowed_cross, total_b, back_mixed
        )
        back_ask, back_key, back_value = (merge_heads(p) for p in (back_ask, back_key, back_value))
        back_normed = swap_sum(matmul_nt(back_ask, cquery_m), pair)
        back_encoder = swap_sum(matmul_nt(back_key, ckey_m) + matmul_nt(back_value, cvalue_m), pair)
        cross_sum = reduced(
            (
                matmul_tn(normed_b, back_ask),
                matmul_tn(encoder, back_key),
                matmul_tn(encoder, back_value),
                matmul_tn(sent_b, merge_heads(mixed_b)),
            )
        )
        upstream, gain_b = norm_step(upstream, after_a, gain[1], back_normed)

        sent_a = low(upstream)
        back_mixed = divide_heads(low(matmul(sent_a, out_m)))
        back_query, back_key, back_value, back_scores = attend_back(
            query, key, value, bias, allowed_self, total_a, back_mixed
        )
        back_query, back_key, back_value = (merge_heads(p) for p in (back_query, back_key, back_value))
        back_normed = swap_sum(
            matmul_nt(back_query, query_m) + matmul_nt(back_key, key_m) + matmul_nt(back_value, value_m),
            pair,
        )
        self_sum = reduced(
            (
                matmul_tn(normed_a, back_query),
                matmul_tn(normed_a, back_key),
                matmul_tn(normed_a, back_value),
                matmul_tn(sent_a, merge_heads(mixed_a)),
            )
        )
        upstream, gain_a = norm_step(upstream, residual, gain[0], back_normed)

        table_sum = butterfly(table_gradient(bucket, back_scores, bias_table.shape[0]), "dp", count)
        gain_sum = butterfly(jnp.stack([gain_a, gain_b, gain_c]), "dp", count)
        gains_gradient = lax.dynamic_slice(gain_sum, (0, place), (gain_sum.shape[0], width))

        def own_tokens(rows):
            return lax.dynamic_slice_in_dim(rows, half * tokens_here, tokens_here, 0)[None]

        return (
            own_tokens(resid_out),
            own_tokens(upstream),
            own_tokens(back_encoder),
            gains_gradient[None],
            table_sum,
            *[self_sum[i][None] for i in range(4)],
            *[cross_sum[i][None] for i in range(4)],
            *[feed_sum[i][None] for i in range(3)],
        )

    return run


def solution(mesh):
    tokens = P("dp", "tensor", None)
    rows = P("dp", None)
    matrix = P(None, "dp", "tensor")
    gain = P(None, None, ("dp", "tensor"))
    table = P(None, "tensor")
    return jax.shard_map(
        per_device(mesh.shape["dp"], mesh.shape["tensor"]),
        mesh=mesh,
        in_specs=(tokens, tokens, rows, rows, tokens, gain, table) + (matrix,) * 11,
        out_specs=(tokens, tokens, tokens, gain, table) + (matrix,) * 11,
        check_vma=False,
    )
```

```python
import math

import jax
import jax.numpy as jnp
from jax import lax
from jax.experimental import pallas as pl
from jax.experimental.pallas import tpu as pltpu
from jax.sharding import PartitionSpec as P

HEAD_DIM = 64
LANES = 128

epsilon = 1e-06
bucket_steps = [math.ceil(16 * 8 ** (step / 16)) for step in range(1, 16)]
bf16 = jnp.bfloat16
f32 = jnp.float32


def swap(value, bit, count):
    return lax.ppermute(value, "dp", [(i, i ^ bit) for i in range(count)])


def after(value, *earlier):
    return lax.optimization_barrier((value,) + earlier)[0]


def falling_bits(count):
    bits = []
    while count > 1:
        count //= 2
        bits.append(count)
    return bits


def masks(bits):
    found = [0]
    for bit in bits:
        found = found + [bit ^ mask for mask in found]
    return found


def from_all(blocks, order, count):
    place = jnp.zeros((count,), jnp.int32).at[order].set(jnp.arange(count, dtype=jnp.int32))
    sorted_blocks = jnp.take(blocks, place, axis=0)
    parts, columns = blocks.shape[1], blocks.shape[3]
    return jnp.transpose(sorted_blocks, (1, 0, 2, 3)).reshape(1, parts, -1, columns)


def blocks_fit(rows):
    return rows % 16 == 0


def gather_weights(shard, own, count, gate=None):
    buffer = shard[None]
    if count & (count - 1):
        buffer = lax.all_gather(shard, "dp", axis=0)
        order = jnp.arange(count, dtype=jnp.int32)
        return [from_all(buffer, order, count)], jnp.zeros((1,), jnp.int32), buffer
    if gate is not None:
        buffer = after(buffer, gate)
    bits = falling_bits(count)
    first = None
    for bit in bits[:-1]:
        arrived = swap(buffer, bit, count)
        first = arrived if first is None else first
        buffer = jnp.concatenate([buffer, arrived], axis=0)
    other = swap(buffer, bits[-1], count)
    order = own ^ jnp.asarray(masks(bits), jnp.int32)
    if blocks_fit(shard.shape[1]):
        return [buffer, other], order, first
    whole = from_all(jnp.concatenate([buffer, other], axis=0), order, count)
    return [whole], jnp.zeros((1,), jnp.int32), first


def reduce_order(own, count):
    bits = falling_bits(count)
    return own ^ jnp.asarray(masks(bits), jnp.int32)


def reduce_gradients(blocks, own, count):
    if blocks.shape[0] != count:
        parts, columns = blocks.shape[1], blocks.shape[3]
        natural = jnp.transpose(blocks.reshape(parts, count, -1, columns), (1, 0, 2, 3))
        if count & (count - 1):
            return lax.psum_scatter(natural.astype(f32), "dp", scatter_dimension=0, tiled=True)[0]
        blocks = jnp.take(natural, reduce_order(own, count), axis=0)
    terms = [blocks]
    bit = 1
    extent = count
    while extent > 1:
        half = extent // 2
        sent = sum(term[half:extent].astype(f32) for term in terms).astype(bf16)
        terms.append(swap(sent, bit, count))
        bit *= 2
        extent = half
    return sum(term[0].astype(f32) for term in terms)


def butterfly(value, axis, count):
    if count & (count - 1):
        return lax.psum(value, axis)
    step = 1
    while step < count:
        value = value + lax.ppermute(value, axis, [(i, i ^ step) for i in range(count)])
        step *= 2
    return value


def from_pair(value):
    return lax.ppermute(value, "tensor", [(0, 1), (1, 0)])


def gather_tokens(rows, half):
    other = from_pair(rows)
    first = half == 0
    return jnp.concatenate([jnp.where(first, rows, other), jnp.where(first, other, rows)], axis=0)


def dot(left, right):
    return jnp.dot(left, right, preferred_element_type=f32)


def dot_nt(left, right):
    return lax.dot_general(left, right, (((1,), (1,)), ((), ())), preferred_element_type=f32)


def dot_tn(left, right):
    return lax.dot_general(left, right, (((0,), (0,)), ((), ())), preferred_element_type=f32)


def inverse_rms(rows):
    return lax.rsqrt(jnp.mean(rows * rows, axis=-1, keepdims=True) + epsilon)


def norm_back(rows, gain, gradient):
    inverse = inverse_rms(rows)
    scaled = gradient * gain
    lean = jnp.mean(scaled * rows, axis=-1, keepdims=True)
    back = inverse * scaled - rows * (inverse * inverse * inverse * lean)
    return back, jnp.sum(gradient * (rows * inverse), axis=0, keepdims=True)


def place_blocks(order_ref, buffers, matrices_ref):
    rows = buffers[0].shape[2]
    index = 0
    for buffer in buffers:
        for block in range(buffer.shape[0]):
            start = pl.multiple_of(order_ref[index] * rows, 16)
            matrices_ref[:, pl.ds(start, rows), :] = buffer[block]
            index += 1


def store_blocks(order_ref, gradient_ref, out_ref, part):
    rows = out_ref.shape[2]
    for block in range(out_ref.shape[0]):
        start = pl.multiple_of(order_ref[block] * rows, 16)
        out_ref[block, part] = gradient_ref[pl.ds(start, rows), :].astype(bf16)


def first_head(shape):
    return lax.broadcasted_iota(jnp.int32, shape, 1) < HEAD_DIM


def only(rows, lanes, member):
    return jnp.where(lanes if member == 0 else jnp.logical_not(lanes), rows, jnp.zeros_like(rows))


def bias_of(line_ref, head, length):
    line = jnp.broadcast_to(line_ref[head : head + 1, :], (length, length))
    return pltpu.roll(line, 0, 1, stride=1, stride_axis=0)


def diagonal_sums(scores):
    length = scores.shape[0]
    total = scores[:8]
    for start in range(8, length, 8):
        total = total + pltpu.roll(scores[start : start + 8], length - start, 1)
    line = total[:1]
    for row in range(1, 8):
        line = line + pltpu.roll(total[row : row + 1], length - row, 1)
    return line


def allowed_pairs(column_ref, row_ref, causal):
    same = column_ref[...] == row_ref[...]
    if not causal:
        return same
    shape = same.shape
    rows = lax.broadcasted_iota(jnp.int32, shape, 0)
    return jnp.logical_and(same, rows >= lax.broadcasted_iota(jnp.int32, shape, 1))


def probabilities(query, key, bias, allowed):
    scores = dot_nt(query, key)
    if bias is not None:
        scores = scores + bias
    scores = jnp.where(allowed, scores, -jnp.inf)
    raised = jnp.exp(scores - jnp.max(scores, axis=-1, keepdims=True))
    return raised / jnp.sum(raised, axis=-1, keepdims=True)


def attend(query_ref, key_ref, value_ref, mixed_ref, allowed, line_ref):
    length, width = query_ref.shape
    lanes = first_head((length, LANES))
    for pair in range(width // LANES):
        at = pl.ds(pair * LANES, LANES)
        query, key, value = query_ref[:, at], key_ref[:, at], value_ref[:, at]
        mixed = []
        for member in range(2):
            bias = None if line_ref is None else bias_of(line_ref, 2 * pair + member, length)
            shares = probabilities(only(query, lanes, member), key, bias, allowed)
            mixed.append(dot(shares.astype(bf16), value))
        mixed_ref[:, at] = jnp.where(lanes, mixed[0], mixed[1]).astype(bf16)


def attend_back(
    query_ref, key_ref, value_ref, back_ref, allowed, line_ref,
    back_query_ref, back_key_ref, back_value_ref, line_back_ref,
):
    length, width = query_ref.shape
    lanes = first_head((length, LANES))
    other_lanes = first_head((key_ref.shape[0], LANES))
    for pair in range(width // LANES):
        at = pl.ds(pair * LANES, LANES)
        query, key, value, back = query_ref[:, at], key_ref[:, at], value_ref[:, at], back_ref[:, at]
        queries, keys, values = [], [], []
        for member in range(2):
            head = 2 * pair + member
            bias = None if line_ref is None else bias_of(line_ref, head, length)
            shares = probabilities(only(query, lanes, member), key, bias, allowed)
            back_shares = dot_nt(only(back, lanes, member), value)
            delta = jnp.sum(shares * back_shares, axis=-1, keepdims=True)
            scores = shares * (back_shares - delta)
            if line_back_ref is not None:
                line_back_ref[head : head + 1, :] = diagonal_sums(scores)
            low = scores.astype(bf16)
            values.append(dot_tn(shares.astype(bf16), back))
            queries.append(dot(low, key))
            keys.append(dot_tn(low, query))
        back_query_ref[:, at] = jnp.where(lanes, queries[0], queries[1]).astype(bf16)
        back_key_ref[:, at] = jnp.where(other_lanes, keys[0], keys[1]).astype(bf16)
        back_value_ref[:, at] = jnp.where(other_lanes, values[0], values[1]).astype(bf16)


def kernel_call(body, outs, inputs, order, buffers, scratch, name):
    number, many = len(inputs), len(buffers)

    def run(order_ref, *refs):
        body(order_ref, refs[:many], *refs[many:])

    vmem = pl.BlockSpec(memory_space=pltpu.VMEM)
    return pl.pallas_call(
        run,
        out_shape=[jax.ShapeDtypeStruct(shape, kind) for shape, kind in outs],
        in_specs=[pl.BlockSpec(memory_space=pltpu.SMEM)] + [vmem] * (many + number),
        out_specs=[vmem] * len(outs),
        scratch_shapes=[pltpu.VMEM(shape, kind) for shape, kind in scratch],
        name=name,
    )(order, *buffers, *inputs)


def matrices_of(buffers):
    parts, rows, columns = buffers[0].shape[1:]
    return (parts, rows * sum(buffer.shape[0] for buffer in buffers), columns)


def self_forward(residual, gain, line, column, row, weights):
    buffers, order = weights
    length, model = residual.shape
    inner = buffers[0].shape[3]

    def body(order_ref, buffers, resid_ref, gain_ref, line_ref, column_ref, row_ref,
             normed_ref, query_ref, key_ref, value_ref, mixed_ref, low_ref, w_ref):
        place_blocks(order_ref, buffers, w_ref)
        rows = resid_ref[...]
        normed = (rows * inverse_rms(rows) * gain_ref[0:1, :]).astype(bf16)
        normed_ref[...] = normed
        query_ref[...] = dot(normed, w_ref[0]).astype(bf16)
        key_ref[...] = dot(normed, w_ref[1]).astype(bf16)
        value_ref[...] = dot(normed, w_ref[2]).astype(bf16)
        allowed = allowed_pairs(column_ref, row_ref, True)
        attend(query_ref, key_ref, value_ref, mixed_ref, allowed, line_ref)
        low_ref[...] = dot_nt(mixed_ref[...], w_ref[3]).astype(bf16)

    heads = ((length, inner), bf16)
    return kernel_call(
        body,
        [((length, model), bf16), heads, heads, heads, heads, ((length, model), bf16)],
        (residual, gain, line, column, row), order, buffers,
        [(matrices_of(buffers), bf16)], "self_forward",
    )


def cross_forward(residual, low, arrived, encoder, gain, column, row, weights):
    buffers, order = weights
    length, model = residual.shape
    far = encoder.shape[0]
    inner = buffers[0].shape[3]

    def body(order_ref, buffers, resid_ref, low_in_ref, arrived_ref, encoder_ref, gain_ref,
             column_ref, row_ref, after_ref, normed_ref, ask_ref, key_ref, value_ref, mixed_ref,
             low_ref, w_ref):
        place_blocks(order_ref, buffers, w_ref)
        rows = resid_ref[...] + (low_in_ref[...].astype(f32) + arrived_ref[...].astype(f32))
        after_ref[...] = rows
        normed = (rows * inverse_rms(rows) * gain_ref[1:2, :]).astype(bf16)
        normed_ref[...] = normed
        ask_ref[...] = dot(normed, w_ref[0]).astype(bf16)
        key_ref[...] = dot(encoder_ref[...], w_ref[1]).astype(bf16)
        value_ref[...] = dot(encoder_ref[...], w_ref[2]).astype(bf16)
        allowed = allowed_pairs(column_ref, row_ref, False)
        attend(ask_ref, key_ref, value_ref, mixed_ref, allowed, None)
        low_ref[...] = dot_nt(mixed_ref[...], w_ref[3]).astype(bf16)

    here, there = ((length, inner), bf16), ((far, inner), bf16)
    wide = ((length, model), bf16)
    return kernel_call(
        body,
        [((length, model), f32), wide, here, there, there, here, wide],
        (residual, low, arrived, encoder, gain, column, row), order, buffers,
        [(matrices_of(buffers), bf16)], "cross_forward",
    )


def feed_both(residual, low, arrived, upstream, gain, weights):
    buffers, order = weights
    length, model = residual.shape
    units = buffers[0].shape[3]
    root = math.sqrt(2.0 / math.pi)

    def body(order_ref, buffers, resid_ref, low_in_ref, arrived_ref, upstream_ref, gain_ref,
             after_ref, normed_ref, sent_ref, hidden_ref, back_gate_ref, back_upper_ref, low_ref,
             back_ref, w_ref):
        place_blocks(order_ref, buffers, w_ref)
        rows = resid_ref[...] + (low_in_ref[...].astype(f32) + arrived_ref[...].astype(f32))
        after_ref[...] = rows
        normed = (rows * inverse_rms(rows) * gain_ref[2:3, :]).astype(bf16)
        normed_ref[...] = normed
        sent = upstream_ref[...].astype(bf16)
        sent_ref[...] = sent
        chunk = min(units, 256)
        total = None
        for start in range(0, units, chunk):
            at = pl.ds(start, chunk)
            gate = dot(normed, w_ref[0, :, at])
            upper = dot(normed, w_ref[1, :, at])
            back_hidden = dot(sent, w_ref[2, :, at])
            square = gate * gate
            bent = jnp.tanh(root * (gate + 0.044715 * (square * gate)))
            part = 0.5 * (1.0 + bent)
            active = gate * part
            slope = part + 0.5 * gate * (1.0 - bent * bent) * (root * (1.0 + 3 * 0.044715 * square))
            hidden_ref[:, at] = (active * upper).astype(bf16)
            back_gate = (back_hidden * upper * slope).astype(bf16)
            back_upper = (back_hidden * active).astype(bf16)
            back_gate_ref[:, at] = back_gate
            back_upper_ref[:, at] = back_upper
        back_ref[...] = (
            dot_nt(back_gate_ref[...], w_ref[0]) + dot_nt(back_upper_ref[...], w_ref[1])
        ).astype(bf16)
        low_ref[...] = dot_nt(hidden_ref[...], w_ref[2]).astype(bf16)

    wide, deep = ((length, model), bf16), ((length, units), bf16)
    return kernel_call(
        body,
        [((length, model), f32), wide, wide, deep, deep, deep, wide, wide],
        (residual, low, arrived, upstream, gain), order, buffers,
        [(matrices_of(buffers), bf16)], "feed_both",
    )


def cross_backward(upstream, rows, low, arrived, gain, ask, key, value, column, row, weights):
    buffers, order = weights
    length, model = upstream.shape
    far, inner = key.shape

    def body(order_ref, buffers, upstream_ref, rows_ref, low_in_ref, arrived_ref, gain_ref, ask_ref,
             key_ref, value_ref, column_ref, row_ref, up_ref, sent_ref, gain_out_ref, back_ask_ref,
             back_key_ref, back_value_ref, low_ref, low_encoder_ref, mixed_ref, w_ref):
        place_blocks(order_ref, buffers, w_ref)
        error = low_in_ref[...].astype(f32) + arrived_ref[...].astype(f32)
        back, gain_row = norm_back(rows_ref[...], gain_ref[2:3, :], error)
        gain_out_ref[...] = gain_row
        total = upstream_ref[...] + back
        up_ref[...] = total
        sent = total.astype(bf16)
        sent_ref[...] = sent
        mixed_ref[...] = dot(sent, w_ref[3]).astype(bf16)
        allowed = allowed_pairs(column_ref, row_ref, False)
        attend_back(ask_ref, key_ref, value_ref, mixed_ref, allowed, None,
                    back_ask_ref, back_key_ref, back_value_ref, None)
        low_ref[...] = dot_nt(back_ask_ref[...], w_ref[0]).astype(bf16)
        low_encoder_ref[...] = (
            dot_nt(back_key_ref[...], w_ref[1]) + dot_nt(back_value_ref[...], w_ref[2])
        ).astype(bf16)

    here, there = ((length, inner), bf16), ((far, inner), bf16)
    wide = ((length, model), bf16)
    return kernel_call(
        body,
        [((length, model), f32), wide, ((1, model), f32), here, there, there, wide,
         ((far, model), bf16)],
        (upstream, rows, low, arrived, gain, ask, key, value, column, row), order, buffers,
        [here, (matrices_of(buffers), bf16)], "cross_backward",
    )


def self_backward(upstream, rows, low, arrived, gain, query, key, value, line, column, row, weights):
    buffers, order = weights
    length, model = upstream.shape
    inner = key.shape[1]

    def body(order_ref, buffers, upstream_ref, rows_ref, low_in_ref, arrived_ref, gain_ref, query_ref,
             key_ref, value_ref, line_ref, column_ref, row_ref, up_ref, sent_ref, gain_out_ref,
             back_query_ref, back_key_ref, back_value_ref, low_ref, line_out_ref, mixed_ref, w_ref):
        place_blocks(order_ref, buffers, w_ref)
        error = low_in_ref[...].astype(f32) + arrived_ref[...].astype(f32)
        back, gain_row = norm_back(rows_ref[...], gain_ref[1:2, :], error)
        gain_out_ref[...] = gain_row
        total = upstream_ref[...] + back
        up_ref[...] = total
        sent = total.astype(bf16)
        sent_ref[...] = sent
        mixed_ref[...] = dot(sent, w_ref[3]).astype(bf16)
        allowed = allowed_pairs(column_ref, row_ref, True)
        attend_back(query_ref, key_ref, value_ref, mixed_ref, allowed, line_ref,
                    back_query_ref, back_key_ref, back_value_ref, line_out_ref)
        low_ref[...] = (
            dot_nt(back_query_ref[...], w_ref[0])
            + dot_nt(back_key_ref[...], w_ref[1])
            + dot_nt(back_value_ref[...], w_ref[2])
        ).astype(bf16)

    here, wide = ((length, inner), bf16), ((length, model), bf16)
    return kernel_call(
        body,
        [((length, model), f32), wide, ((1, model), f32), here, here, here, wide,
         (line.shape, f32)],
        (upstream, rows, low, arrived, gain, query, key, value, line, column, row), order, buffers,
        [here, (matrices_of(buffers), bf16)], "self_backward",
    )


def weight_gradients(pairs, order, count, name):
    model, columns = pairs[0][0].shape[1], pairs[0][1].shape[1]
    inputs = []
    places = []
    for left, right in pairs:
        for value in (left, right):
            if not any(value is known for known in inputs):
                inputs.append(value)
        places.append(tuple(next(i for i, k in enumerate(inputs) if k is v) for v in (left, right)))
    number = len(inputs)
    fits = blocks_fit(model // count)
    blocks = count if fits else 1

    def body(order_ref, buffers, *refs):
        out_ref, scratch_ref = refs[number], refs[number + 1]
        for part, (left, right) in enumerate(places):
            scratch_ref[...] = dot_tn(refs[left][...], refs[right][...])
            store_blocks(order_ref, scratch_ref, out_ref, part)

    return kernel_call(
        body,
        [((blocks, len(pairs), model // blocks, columns), bf16)],
        tuple(inputs), order if fits else jnp.zeros((1,), jnp.int32), [],
        [((model, columns), f32)], name,
    )[0]


def bucket_of(distance):
    beyond = jnp.full(distance.shape, 16, jnp.int32)
    for edge in bucket_steps:
        beyond = beyond + (distance >= edge).astype(jnp.int32)
    return jnp.where(distance < 16, distance, beyond)


def per_device(count):
    def run(
        resid_in, encoded, dec_segments, enc_segments, out_grad, gains, bias_table,
        self_query, self_key, self_value, self_out,
        cross_query, cross_key, cross_value, cross_out,
        ff_gate, ff_up, ff_down,
    ):
        tokens_here = resid_in.shape[1]
        length = dec_segments.shape[1]
        half = lax.axis_index("tensor")
        own = lax.axis_index("dp")
        order = reduce_order(own, count)
        stack = lambda *matrices: jnp.concatenate(matrices, axis=0)

        buffers, places, gate = gather_weights(
            stack(self_query, self_key, self_value, self_out), own, count
        )
        self_weights = (buffers, places)
        residual = gather_tokens(resid_in[0], half)

        width = gains.shape[2]
        place = (own * 2 + half) * width
        gain = lax.dynamic_update_slice(
            jnp.zeros((gains.shape[1], width * count * 2), f32), gains[0], (0, place)
        )
        gain = butterfly(butterfly(gain, "tensor", 2), "dp", count)

        buffers, places, gate = gather_weights(
            stack(cross_query, cross_key, cross_value, cross_out), own, count, gate
        )
        cross_weights = (buffers, places)
        encoder = gather_tokens(encoded[0], half)
        buffers, places, gate = gather_weights(stack(ff_gate, ff_up, ff_down), own, count, gate)
        feed_weights = (buffers, places)
        upstream = gather_tokens(out_grad[0], half)

        labels = lax.broadcasted_iota(jnp.int32, (bias_table.shape[0], 1), 0)
        turned = (length - lax.broadcasted_iota(jnp.int32, (1, length), 1)) % length
        line = jnp.einsum(
            "bh,bk->hk", bias_table, (bucket_of(turned) == labels).astype(f32),
            precision=lax.Precision.HIGHEST,
        )
        dec_row, enc_row = dec_segments[:1], enc_segments[:1]
        dec_column = dec_row.reshape(-1, 1)

        normed_a, query, key, value, mixed_a, low_a = self_forward(
            residual, gain, line, dec_column, dec_row, self_weights
        )
        after_a, normed_b, ask, key_cross, value_cross, mixed_b, low_b = cross_forward(
            residual, low_a, from_pair(low_a), encoder, gain, dec_column, enc_row, cross_weights
        )
        after_b, normed_c, sent_c, hidden, back_gate, back_upper, low_c, low_d = feed_both(
            after_a, low_b, from_pair(low_b), upstream, gain, feed_weights
        )
        arrived_d = from_pair(low_d)
        feed_blocks = weight_gradients(
            ((normed_c, back_gate), (normed_c, back_upper), (sent_c, hidden)), order, count, "feed_weights"
        )
        feed_sum = reduce_gradients(feed_blocks, own, count)

        up_b, sent_b, gain_c, back_ask, back_key, back_value, low_e, low_encoder = cross_backward(
            upstream, after_b, low_d, arrived_d, gain, ask, key_cross, value_cross,
            dec_column, enc_row, cross_weights,
        )
        arrived_e = from_pair(low_e)
        cross_blocks = weight_gradients(
            ((normed_b, back_ask), (encoder, back_key), (encoder, back_value), (sent_b, mixed_b)),
            order, count, "cross_weights",
        )
        cross_sum = reduce_gradients(cross_blocks, own, count)

        up_a, sent_a, gain_b, back_query, back_key, back_value, low_f, line_back = self_backward(
            up_b, after_a, low_e, arrived_e, gain, query, key, value, line,
            dec_column, dec_row, self_weights,
        )
        self_blocks = weight_gradients(
            ((normed_a, back_query), (normed_a, back_key), (normed_a, back_value), (sent_a, mixed_a)),
            order, count, "self_weights",
        )
        self_sum = reduce_gradients(self_blocks, own, count)

        def own_tokens(rows):
            return lax.dynamic_slice_in_dim(rows, half * tokens_here, tokens_here, 0)

        def others_tokens(rows):
            return lax.dynamic_slice_in_dim(rows, (1 - half) * tokens_here, tokens_here, 0)

        def own_sum(low):
            return own_tokens(low).astype(f32) + from_pair(others_tokens(low)).astype(f32)

        resid_out = own_tokens(after_b) + own_sum(low_c)
        encoder_gradient = own_sum(low_encoder)
        back, gain_a = norm_back(resid_in[0], gain[0:1], own_sum(low_f))
        input_gradient = own_tokens(up_a) + back

        first = (half == 0).astype(f32)
        small = jnp.concatenate([gain_a, gain_b * first, gain_c * first], axis=0)
        heads = line_back.shape[0]
        small = jnp.concatenate(
            [butterfly(small, "tensor", 2), jnp.pad(line_back, ((0, 0), (0, small.shape[1] - length)))], axis=0
        )
        small = butterfly(small, "dp", count)
        gains_gradient = lax.dynamic_slice(small, (0, place), (3, width))
        table_gradient = jnp.einsum(
            "bk,hk->bh", (bucket_of(turned) == labels).astype(f32), small[3 : 3 + heads, :length],
            precision=lax.Precision.HIGHEST,
        )
        return (
            resid_out[None],
            input_gradient[None],
            encoder_gradient[None],
            gains_gradient[None],
            table_gradient,
            *[self_sum[i][None] for i in range(4)],
            *[cross_sum[i][None] for i in range(4)],
            *[feed_sum[i][None] for i in range(3)],
        )

    return run


def solution(mesh):
    tokens = P("dp", "tensor", None)
    rows = P("dp", None)
    matrix = P(None, "dp", "tensor")
    gain = P(None, None, ("dp", "tensor"))
    table = P(None, "tensor")
    return jax.shard_map(
        per_device(mesh.shape["dp"]),
        mesh=mesh,
        in_specs=(tokens, tokens, rows, rows, tokens, gain, table) + (matrix,) * 11,
        out_specs=(tokens, tokens, tokens, gain, table) + (matrix,) * 11,
        check_vma=False,
    )
```

```python
import math

import jax
import jax.numpy as jnp
from jax import lax
from jax.experimental import pallas as pl
from jax.experimental.pallas import tpu as pltpu
from jax.sharding import PartitionSpec as P


HEAD_DIM = 64
LANES = 128

epsilon = 1e-06
bucket_steps = [math.ceil(16 * 8 ** (step / 16)) for step in range(1, 16)]
bf16 = jnp.bfloat16
f32 = jnp.float32


def swap(value, bit, count):
    return lax.ppermute(value, "dp", [(i, i ^ bit) for i in range(count)])


def gather_bits(count, early):
    bits = []
    while count > 1:
        count //= 2
        bits.append(count)
    if early and len(bits) > 2:
        bits = [bits[-2]] + bits[:-2] + [bits[-1]]
    return bits


def masks(bits):
    found = [0]
    for bit in bits:
        found = found + [bit ^ mask for mask in found]
    return jnp.asarray(found, jnp.int32)


def from_all(blocks, order, count):
    place = jnp.zeros((count,), jnp.int32).at[order].set(jnp.arange(count, dtype=jnp.int32))
    return jnp.take(blocks, place, axis=0).reshape(1, -1, blocks.shape[2])


def blocks_fit(rows):
    return rows % 16 == 0


def gather_weights(matrices, own, count, early=False):
    shard = jnp.concatenate(matrices, axis=1)
    buffer = shard[None]
    if count & (count - 1):
        buffer = lax.all_gather(shard, "dp", axis=0)
        order = jnp.arange(count, dtype=jnp.int32)
        return [from_all(buffer, order, count)], jnp.zeros((1,), jnp.int32)
    bits = gather_bits(count, early)
    for bit in bits[:-1]:
        buffer = jnp.concatenate([buffer, swap(buffer, bit, count)], axis=0)
    other = swap(buffer, bits[-1], count)
    order = own ^ masks(bits)
    if blocks_fit(shard.shape[0]):
        return [buffer, other], order
    whole = from_all(jnp.concatenate([buffer, other], axis=0), order, count)
    return [whole], jnp.zeros((1,), jnp.int32)


def reduce_order(own, count, early):
    return own ^ masks(gather_bits(count, early))


def reduce_gradients(halves, widths, own, count, early=False):
    if len(halves) == 1:
        blocks = halves[0].reshape(count, -1, halves[0].shape[2])
        if count & (count - 1):
            summed = lax.psum_scatter(blocks.astype(f32), "dp", scatter_dimension=0, tiled=True)[0]
            return jnp.split(summed, [sum(widths[:i]) for i in range(1, len(widths))], axis=1)
        blocks = jnp.take(blocks, reduce_order(own, count, early), axis=0)
        halves = (blocks[: count // 2], blocks[count // 2 :])
    kept, sent = halves
    terms = [kept]
    extent = count // 2
    for step, bit in enumerate(reversed(gather_bits(count, early))):
        if step > 0:
            half = extent // 2
            sent = sum(term[half:extent].astype(f32) for term in terms).astype(bf16)
            extent = half
        terms.append(swap(sent, bit, count))
    found = []
    start = 0
    for width in widths:
        found.append(sum(term[0, :, start : start + width].astype(f32) for term in terms))
        start += width
    return found


def from_pair(value):
    return lax.ppermute(value, "tensor", [(0, 1), (1, 0)])


def dot(left, right):
    return jnp.dot(left, right, preferred_element_type=f32)


def dot_nt(left, right):
    return lax.dot_general(left, right, (((1,), (1,)), ((), ())), preferred_element_type=f32)


def dot_tn(left, right):
    return lax.dot_general(left, right, (((0,), (0,)), ((), ())), preferred_element_type=f32)


def inverse_rms(rows):
    return lax.rsqrt(jnp.mean(rows * rows, axis=-1, keepdims=True) + epsilon)


def norm_back(rows, gain, gradient):
    inverse = inverse_rms(rows)
    scaled = gradient * gain
    lean = jnp.mean(scaled * rows, axis=-1, keepdims=True)
    return inverse * scaled - rows * (inverse * inverse * inverse * lean)


def gain_row(rows, part):
    return jnp.sum(part * (rows * inverse_rms(rows)), axis=0, keepdims=True)


def place_blocks(order_ref, buffers, matrices_ref):
    rows = buffers[0].shape[1]
    index = 0
    for buffer in buffers:
        for block in range(buffer.shape[0]):
            start = pl.multiple_of(order_ref[index] * rows, 16)
            matrices_ref[pl.ds(start, rows), :] = buffer[block]
            index += 1


def store_blocks(order_ref, gradient_ref, out_refs, start, width):
    index = 0
    for out_ref in out_refs:
        rows = out_ref.shape[1]
        for block in range(out_ref.shape[0]):
            row = pl.multiple_of(order_ref[index] * rows, 16)
            out_ref[block, :, start : start + width] = gradient_ref[pl.ds(row, rows), :width].astype(bf16)
            index += 1


def join_halves(half_ref, own_ref, other_ref, out_ref):
    tokens = own_ref.shape[0]
    half = half_ref[0]
    out_ref[pl.ds(pl.multiple_of(half * tokens, 16), tokens), :] = own_ref[...]
    out_ref[pl.ds(pl.multiple_of((1 - half) * tokens, 16), tokens), :] = other_ref[...]


def part_halves(half_ref, low_ref, kept_ref, sent_ref, start):
    tokens = low_ref.shape[0] // 2
    half = half_ref[0]
    at = pl.ds(start, tokens)
    kept_ref[at, :] = low_ref[pl.ds(pl.multiple_of(half * tokens, 16), tokens), :]
    sent_ref[at, :] = low_ref[pl.ds(pl.multiple_of((1 - half) * tokens, 16), tokens), :]


def first_head(shape):
    return lax.broadcasted_iota(jnp.int32, shape, 1) < HEAD_DIM


def only(rows, lanes, member):
    return jnp.where(lanes if member == 0 else jnp.logical_not(lanes), rows, jnp.zeros_like(rows))


def bias_of(line_ref, head, length):
    line = jnp.broadcast_to(line_ref[head : head + 1, :], (length, length))
    return pltpu.roll(line, 0, 1, stride=1, stride_axis=0)


def diagonal_sums(scores):
    length = scores.shape[0]
    total = scores[:8]
    for start in range(8, length, 8):
        total = total + pltpu.roll(scores[start : start + 8], length - start, 1)
    line = total[:1]
    for row in range(1, 8):
        line = line + pltpu.roll(total[row : row + 1], length - row, 1)
    return line


def allowed_pairs(column_ref, row_ref, causal):
    same = column_ref[...] == row_ref[...]
    if not causal:
        return same
    shape = same.shape
    rows = lax.broadcasted_iota(jnp.int32, shape, 0)
    return jnp.logical_and(same, rows >= lax.broadcasted_iota(jnp.int32, shape, 1))


def probabilities(query, key, bias, allowed):
    scores = dot_nt(query, key)
    if bias is not None:
        scores = scores + bias
    scores = jnp.where(allowed, scores, -jnp.inf)
    raised = jnp.exp(scores - jnp.max(scores, axis=-1, keepdims=True))
    return raised / jnp.sum(raised, axis=-1, keepdims=True)


def attend(query_ref, key_ref, value_ref, mixed_ref, allowed, line_ref):
    length, width = query_ref.shape
    lanes = first_head((length, LANES))
    for pair in range(width // LANES):
        at = pl.ds(pair * LANES, LANES)
        query, key, value = query_ref[:, at], key_ref[:, at], value_ref[:, at]
        mixed = []
        for member in range(2):
            bias = None if line_ref is None else bias_of(line_ref, 2 * pair + member, length)
            shares = probabilities(only(query, lanes, member), key, bias, allowed)
            mixed.append(dot(shares.astype(bf16), value))
        mixed_ref[:, at] = jnp.where(lanes, mixed[0], mixed[1]).astype(bf16)


def attend_back(
    query_ref, key_ref, value_ref, back_ref, allowed, line_ref,
    back_query_ref, back_key_ref, back_value_ref, line_back_ref,
):
    length, width = query_ref.shape
    lanes = first_head((length, LANES))
    other_lanes = first_head((key_ref.shape[0], LANES))
    for pair in range(width // LANES):
        at = pl.ds(pair * LANES, LANES)
        query, key, value, back = query_ref[:, at], key_ref[:, at], value_ref[:, at], back_ref[:, at]
        queries, keys, values = [], [], []
        for member in range(2):
            head = 2 * pair + member
            bias = None if line_ref is None else bias_of(line_ref, head, length)
            shares = probabilities(only(query, lanes, member), key, bias, allowed)
            back_shares = dot_nt(only(back, lanes, member), value)
            delta = jnp.sum(shares * back_shares, axis=-1, keepdims=True)
            scores = shares * (back_shares - delta)
            if line_back_ref is not None:
                line_back_ref[head : head + 1, :] = diagonal_sums(scores)
            low = scores.astype(bf16)
            values.append(dot_tn(shares.astype(bf16), back))
            queries.append(dot(low, key))
            keys.append(dot_tn(low, query))
        back_query_ref[:, at] = jnp.where(lanes, queries[0], queries[1]).astype(bf16)
        back_key_ref[:, at] = jnp.where(other_lanes, keys[0], keys[1]).astype(bf16)
        back_value_ref[:, at] = jnp.where(other_lanes, values[0], values[1]).astype(bf16)


def kernel_call(body, outs, inputs, orders, groups, scratch):
    buffers = [buffer for group in groups for buffer in group]

    def run(*refs):
        refs = list(refs)
        order_refs, refs = refs[: len(orders)], refs[len(orders) :]
        held = []
        for group in groups:
            held.append(refs[: len(group)])
            refs = refs[len(group) :]
        body(order_refs, held, *refs)

    vmem = pl.BlockSpec(memory_space=pltpu.VMEM)
    return pl.pallas_call(
        run,
        out_shape=[jax.ShapeDtypeStruct(shape, kind) for shape, kind in outs],
        in_specs=[pl.BlockSpec(memory_space=pltpu.SMEM)] * len(orders)
        + [vmem] * (len(buffers) + len(inputs)),
        out_specs=[vmem] * len(outs),
        scratch_shapes=[pltpu.VMEM(shape, kind) for shape, kind in scratch],
    )(*orders, *buffers, *inputs)


def matrices_of(buffers):
    rows, columns = buffers[0].shape[1:]
    return (rows * sum(buffer.shape[0] for buffer in buffers), columns)


def column(matrices_ref, index, width):
    return matrices_ref[:, index * width : (index + 1) * width]


def self_forward(half, rows, other, line, column_ids, row_ids, inner, weights):
    (buffers, order), (last_buffers, last_order) = weights
    length, model = 2 * rows.shape[0], rows.shape[1]

    def body(orders, groups, own_ref, other_ref, line_ref, column_ref, row_ref,
             resid_ref, gain_ref, normed_ref, query_ref, key_ref, value_ref, mixed_ref, low_ref,
             w_ref, last_ref):
        place_blocks(orders[0], groups[0], w_ref)
        place_blocks(orders[1], groups[1], last_ref)
        pieces = jnp.transpose(last_ref[:, 2 * inner :].astype(f32))
        gain = pieces[0:3] + pieces[3:6] + pieces[6:9]
        gain_ref[...] = gain
        join_halves(orders[2], own_ref, other_ref, resid_ref)
        rows = resid_ref[...]
        normed = (rows * inverse_rms(rows) * gain[0:1, :]).astype(bf16)
        normed_ref[...] = normed
        query_ref[...] = dot(normed, column(w_ref, 0, inner)).astype(bf16)
        key_ref[...] = dot(normed, column(w_ref, 1, inner)).astype(bf16)
        value_ref[...] = dot(normed, column(last_ref, 0, inner)).astype(bf16)
        allowed = allowed_pairs(column_ref, row_ref, True)
        attend(query_ref, key_ref, value_ref, mixed_ref, allowed, line_ref)
        low_ref[...] = dot_nt(mixed_ref[...], column(last_ref, 1, inner)).astype(bf16)

    heads, wide = ((length, inner), bf16), ((length, model), bf16)
    return kernel_call(
        body,
        [((length, model), f32), ((3, model), f32), wide, heads, heads, heads, heads, wide],
        (rows, other, line, column_ids, row_ids), [order, last_order, half], [buffers, last_buffers],
        [(matrices_of(buffers), bf16), (matrices_of(last_buffers), bf16)],
    )


def cross_forward(half, residual, low, arrived, encoded, other, gain, column_ids, row_ids, weights):
    buffers, order = weights
    length, model = residual.shape
    far = 2 * encoded.shape[0]
    inner = buffers[0].shape[2] // 4

    def body(orders, groups, resid_ref, low_in_ref, arrived_ref, encoded_ref, other_ref, gain_ref,
             column_ref, row_ref, encoder_ref, after_ref, normed_ref, ask_ref, key_ref, value_ref,
             mixed_ref, low_ref, w_ref):
        place_blocks(orders[0], groups[0], w_ref)
        join_halves(orders[1], encoded_ref, other_ref, encoder_ref)
        rows = resid_ref[...] + (low_in_ref[...].astype(f32) + arrived_ref[...].astype(f32))
        after_ref[...] = rows
        normed = (rows * inverse_rms(rows) * gain_ref[1:2, :]).astype(bf16)
        normed_ref[...] = normed
        ask_ref[...] = dot(normed, column(w_ref, 0, inner)).astype(bf16)
        key_ref[...] = dot(encoder_ref[...], column(w_ref, 1, inner)).astype(bf16)
        value_ref[...] = dot(encoder_ref[...], column(w_ref, 2, inner)).astype(bf16)
        allowed = allowed_pairs(column_ref, row_ref, False)
        attend(ask_ref, key_ref, value_ref, mixed_ref, allowed, None)
        low_ref[...] = dot_nt(mixed_ref[...], column(w_ref, 3, inner)).astype(bf16)

    here, there = ((length, inner), bf16), ((far, inner), bf16)
    wide = ((length, model), bf16)
    return kernel_call(
        body,
        [((far, model), bf16), ((length, model), f32), wide, here, there, there, here, wide],
        (residual, low, arrived, encoded, other, gain, column_ids, row_ids), [order, half], [buffers],
        [(matrices_of(buffers), bf16)],
    )


def feed_both(half, residual, low, arrived, out_grad, other, gain, weights):
    (buffers, order), (down_buffers, down_order) = weights
    length, model = residual.shape
    units = buffers[0].shape[2] // 2
    root = math.sqrt(2.0 / math.pi)

    def body(orders, groups, resid_ref, low_in_ref, arrived_ref, own_ref, other_ref, gain_ref,
             upstream_ref, after_ref, normed_ref, sent_ref, hidden_ref, back_gate_ref, back_upper_ref, low_ref,
             back_ref, w_ref, down_ref):
        place_blocks(orders[0], groups[0], w_ref)
        place_blocks(orders[1], groups[1], down_ref)
        rows = resid_ref[...] + (low_in_ref[...].astype(f32) + arrived_ref[...].astype(f32))
        after_ref[...] = rows
        normed = (rows * inverse_rms(rows) * gain_ref[2:3, :]).astype(bf16)
        normed_ref[...] = normed
        join_halves(orders[2], own_ref, other_ref, upstream_ref)
        sent = upstream_ref[...].astype(bf16)
        sent_ref[...] = sent
        chunk = min(units, 256)
        for start in range(0, units, chunk):
            at = pl.ds(start, chunk)
            gate = dot(normed, w_ref[:, pl.ds(start, chunk)])
            upper = dot(normed, w_ref[:, pl.ds(units + start, chunk)])
            back_hidden = dot(sent, down_ref[:, at])
            square = gate * gate
            bent = jnp.tanh(root * (gate + 0.044715 * (square * gate)))
            part = 0.5 * (1.0 + bent)
            active = gate * part
            slope = part + 0.5 * gate * (1.0 - bent * bent) * (root * (1.0 + 3 * 0.044715 * square))
            hidden_ref[:, at] = (active * upper).astype(bf16)
            back_gate = (back_hidden * upper * slope).astype(bf16)
            back_upper = (back_hidden * active).astype(bf16)
            back_gate_ref[:, at] = back_gate
            back_upper_ref[:, at] = back_upper
        back_ref[...] = (
            dot_nt(back_gate_ref[...], column(w_ref, 0, units))
            + dot_nt(back_upper_ref[...], column(w_ref, 1, units))
        ).astype(bf16)
        low_ref[...] = dot_nt(hidden_ref[...], down_ref[...]).astype(bf16)

    wide, deep = ((length, model), bf16), ((length, units), bf16)
    return kernel_call(
        body,
        [((length, model), f32), ((length, model), f32), wide, wide, deep, deep, deep, wide, wide],
        (residual, low, arrived, out_grad, other, gain), [order, down_order, half], [buffers, down_buffers],
        [(matrices_of(buffers), bf16), (matrices_of(down_buffers), bf16)],
    )


def cross_backward(
    half, upstream, rows, low, arrived, low_feed, gain, ask, key, value, column_ids, row_ids, weights
):
    buffers, order = weights
    length, model = upstream.shape
    far, inner = key.shape
    tokens, far_tokens = length // 2, far // 2

    def body(orders, groups, upstream_ref, rows_ref, low_in_ref, arrived_ref, feed_ref, gain_ref, ask_ref,
             key_ref, value_ref, column_ref, row_ref, up_ref, sent_ref, gain_out_ref, back_ask_ref,
             back_key_ref, back_value_ref, low_ref, out_kept_ref, out_sent_ref, mixed_ref, encoder_ref,
             w_ref):
        place_blocks(orders[0], groups[0], w_ref)
        part = low_in_ref[...].astype(f32)
        rows = rows_ref[...]
        gain_out_ref[...] = gain_row(rows, part)
        total = upstream_ref[...] + norm_back(rows, gain_ref[2:3, :], part + arrived_ref[...].astype(f32))
        up_ref[...] = total
        sent = total.astype(bf16)
        sent_ref[...] = sent
        mixed_ref[...] = dot(sent, column(w_ref, 3, inner)).astype(bf16)
        allowed = allowed_pairs(column_ref, row_ref, False)
        attend_back(ask_ref, key_ref, value_ref, mixed_ref, allowed, None,
                    back_ask_ref, back_key_ref, back_value_ref, None)
        low_ref[...] = dot_nt(back_ask_ref[...], column(w_ref, 0, inner)).astype(bf16)
        encoder_ref[...] = (
            dot_nt(back_key_ref[...], column(w_ref, 1, inner))
            + dot_nt(back_value_ref[...], column(w_ref, 2, inner))
        ).astype(bf16)
        part_halves(orders[1], feed_ref, out_kept_ref, out_sent_ref, 0)
        part_halves(orders[1], encoder_ref, out_kept_ref, out_sent_ref, tokens)

    here, there = ((length, inner), bf16), ((far, inner), bf16)
    wide, both = ((length, model), bf16), ((tokens + far_tokens, model), bf16)
    return kernel_call(
        body,
        [((length, model), f32), wide, ((1, model), f32), here, there, there, wide, both, both],
        (upstream, rows, low, arrived, low_feed, gain, ask, key, value, column_ids, row_ids),
        [order, half], [buffers],
        [here, ((far, model), bf16), (matrices_of(buffers), bf16)],
    )


def self_backward(
    half, upstream, rows, residual, low, arrived, gain, query, key, value, line, column_ids, row_ids, weights
):
    (buffers, order), (last_buffers, last_order) = weights
    length, model = upstream.shape
    inner = key.shape[1]

    def body(orders, groups, upstream_ref, rows_ref, resid_ref, low_in_ref, arrived_ref, gain_ref,
             query_ref, key_ref, value_ref, line_ref, column_ref, row_ref, up_ref, sent_ref, gain_out_ref,
             back_query_ref, back_key_ref, back_value_ref, kept_ref, out_sent_ref, line_out_ref,
             mixed_ref, low_ref, w_ref, last_ref):
        place_blocks(orders[0], groups[0], w_ref)
        place_blocks(orders[1], groups[1], last_ref)
        part = low_in_ref[...].astype(f32)
        rows = rows_ref[...]
        gain_out_ref[1:2, :] = gain_row(rows, part)
        total = upstream_ref[...] + norm_back(rows, gain_ref[1:2, :], part + arrived_ref[...].astype(f32))
        up_ref[...] = total
        sent = total.astype(bf16)
        sent_ref[...] = sent
        mixed_ref[...] = dot(sent, column(last_ref, 1, inner)).astype(bf16)
        allowed = allowed_pairs(column_ref, row_ref, True)
        attend_back(query_ref, key_ref, value_ref, mixed_ref, allowed, line_ref,
                    back_query_ref, back_key_ref, back_value_ref, line_out_ref)
        low = (
            dot_nt(back_query_ref[...], column(w_ref, 0, inner))
            + dot_nt(back_key_ref[...], column(w_ref, 1, inner))
            + dot_nt(back_value_ref[...], column(last_ref, 0, inner))
        ).astype(bf16)
        low_ref[...] = low
        gain_out_ref[0:1, :] = gain_row(resid_ref[...], low.astype(f32))
        part_halves(orders[2], low_ref, kept_ref, out_sent_ref, 0)

    here, wide = ((length, inner), bf16), ((length, model), bf16)
    tokens = ((length // 2, model), bf16)
    return kernel_call(
        body,
        [((length, model), f32), wide, ((2, model), f32), here, here, here, tokens, tokens,
         (line.shape, f32)],
        (upstream, rows, residual, low, arrived, gain, query, key, value, line, column_ids, row_ids),
        [order, last_order, half], [buffers, last_buffers],
        [here, wide, (matrices_of(buffers), bf16), (matrices_of(last_buffers), bf16)],
    )


def finish(half, after_b, up_a, resid_in, kept, arrived, kept_a, arrived_a, gain):
    tokens, model = resid_in.shape
    far_tokens = kept.shape[0] - tokens

    def body(orders, groups, after_ref, up_ref, resid_ref, kept_ref, arrived_ref, kept_a_ref,
             arrived_a_ref, gain_ref, resid_out_ref, input_ref, encoder_ref):
        own = pl.ds(pl.multiple_of(orders[0][0] * tokens, 16), tokens)
        both = kept_ref[...].astype(f32) + arrived_ref[...].astype(f32)
        resid_out_ref[...] = after_ref[own, :] + both[:tokens]
        encoder_ref[...] = both[tokens:]
        error = kept_a_ref[...].astype(f32) + arrived_a_ref[...].astype(f32)
        input_ref[...] = up_ref[own, :] + norm_back(resid_ref[...], gain_ref[0:1, :], error)

    mine = ((tokens, model), f32)
    return kernel_call(
        body, [mine, mine, ((far_tokens, model), f32)],
        (after_b, up_a, resid_in, kept, arrived, kept_a, arrived_a, gain), [half], [], [],
    )


def weight_gradients(groups, orders, count, extra=()):
    model = groups[0][0][0].shape[1]
    inputs = []
    places = []
    for pairs in groups:
        for left, right in pairs:
            for value in (left, right):
                if not any(value is known for known in inputs):
                    inputs.append(value)
        find = lambda value: next(i for i, known in enumerate(inputs) if known is value)
        places.append([(find(left), find(right), right.shape[1]) for left, right in pairs])
    plain = len(inputs)
    inputs = inputs + list(extra)
    number = len(inputs)
    rows = model // count
    fits = blocks_fit(rows)
    blocks = count if fits else 1
    outs = 2 if fits else 1
    widths = [sum(width for unused, unused, width in pairs) for pairs in places]
    if extra:
        widths[-1] += LANES
    widest = max(width for pairs in places for unused, unused, width in pairs)

    def body(orders, unused, *refs):
        scratch_ref = refs[number + outs * len(places)]
        for group, pairs in enumerate(places):
            out_refs = refs[number + outs * group : number + outs * (group + 1)]
            start = 0
            for left, right, width in pairs:
                scratch_ref[:, :width] = dot_tn(refs[left][...], refs[right][...])
                store_blocks(orders[group], scratch_ref, out_refs, start, width)
                start += width
            if extra and group == len(places) - 1:
                last_ref, first_ref, line_ref, bucket_ref = refs[plain:number]
                rows_ref = refs[-1]
                rows_ref[...] = jnp.zeros(rows_ref.shape, f32)
                rows_ref[0:2, :] = first_ref[...]
                rows_ref[2:3, :] = last_ref[...]
                scratch_ref[:, :LANES] = jnp.transpose(rows_ref[...])
                table = lax.dot_general(
                    line_ref[...], bucket_ref[...], (((1,), (0,)), ((), ())),
                    precision=lax.Precision.HIGHEST, preferred_element_type=f32,
                )
                heads = table.shape[0]
                for block in range(count):
                    at = slice(block * rows, block * rows + heads)
                    scratch_ref[at, :LANES] = scratch_ref[at, :LANES] + table
                store_blocks(orders[group], scratch_ref, out_refs, start, LANES)

    found = kernel_call(
        body,
        [((blocks // outs, model // blocks, width), bf16) for width in widths for _ in range(outs)],
        tuple(inputs), list(orders) if fits else [jnp.zeros((1,), jnp.int32)] * len(groups), [],
        [((model, widest), f32)] + ([((LANES, model), f32)] if extra else []),
    )
    return [found[outs * group : outs * (group + 1)] for group in range(len(groups))]


def bucket_of(distance):
    beyond = jnp.full(distance.shape, 16, jnp.int32)
    for edge in bucket_steps:
        beyond = beyond + (distance >= edge).astype(jnp.int32)
    return jnp.where(distance < 16, distance, beyond)


def per_device(count):
    def layer(
        resid_in, encoded, dec_segments, enc_segments, out_grad, gains, bias_table,
        self_query, self_key, self_value, self_out,
        cross_query, cross_key, cross_value, cross_out,
        ff_gate, ff_up, ff_down,
    ):
        length = dec_segments.shape[1]
        half = lax.axis_index("tensor")
        half_here = half.astype(jnp.int32)[None]
        own = lax.axis_index("dp")
        late, early = reduce_order(own, count, False), reduce_order(own, count, True)
        inner, units = self_query.shape[2], ff_gate.shape[2]

        width = gains.shape[2]
        gain_other = from_pair(gains[0])
        first = half == 0
        gain_here = jnp.concatenate(
            [jnp.where(first, gains[0], gain_other), jnp.where(first, gain_other, gains[0])], axis=1
        )
        high = lax.reduce_precision(gain_here, 8, 7)
        middle = lax.reduce_precision(gain_here - high, 8, 7)
        pieces = jnp.concatenate([high, middle, gain_here - high - middle], axis=0).astype(bf16)
        pieces = jnp.pad(jnp.transpose(pieces), ((0, 0), (0, LANES - pieces.shape[0])))

        self_weights = (
            gather_weights((self_query[0], self_key[0]), own, count),
            gather_weights((self_value[0], self_out[0], pieces), own, count),
        )
        cross_weights = gather_weights((cross_query[0], cross_key[0], cross_value[0], cross_out[0]), own, count)
        feed_weights = (
            gather_weights((ff_gate[0], ff_up[0]), own, count), gather_weights((ff_down[0],), own, count, early=True)
        )
        resid_other = from_pair(resid_in[0])
        encoded_other = from_pair(encoded[0])
        out_grad_other = from_pair(out_grad[0])

        buckets = bias_table.shape[0]
        turned = (length - lax.broadcasted_iota(jnp.int32, (1, length), 1)) % length
        line = jnp.einsum(
            "bh,bk->hk", bias_table,
            (bucket_of(turned) == lax.broadcasted_iota(jnp.int32, (buckets, 1), 0)).astype(f32),
            precision=lax.Precision.HIGHEST,
        )
        bucket_lanes = (
            bucket_of(turned).reshape(-1, 1) + buckets == lax.broadcasted_iota(jnp.int32, (1, LANES), 1)
        ).astype(f32)
        dec_row, enc_row = dec_segments[:1], enc_segments[:1]
        dec_column = dec_row.reshape(-1, 1)

        residual, gain, normed_a, query, key, value, mixed_a, low_a = self_forward(
            half_here, resid_in[0], resid_other, line, dec_column, dec_row, inner, self_weights
        )
        encoder, after_a, normed_b, ask, key_cross, value_cross, mixed_b, low_b = cross_forward(
            half_here, residual, low_a, from_pair(low_a), encoded[0], encoded_other, gain,
            dec_column, enc_row, cross_weights,
        )
        upstream, after_b, normed_c, sent_c, hidden, back_gate, back_upper, low_c, low_d = feed_both(
            half_here, after_a, low_b, from_pair(low_b), out_grad[0], out_grad_other, gain,
            feed_weights,
        )
        arrived_d = from_pair(low_d)
        (gate_up,) = weight_gradients((((normed_c, back_gate), (normed_c, back_upper)),), (late,), count)
        (down,) = weight_gradients((((sent_c, hidden),),), (early,), count)
        feed_sum = (
            *reduce_gradients(gate_up, (units, units), own, count),
            *reduce_gradients(down, (units,), own, count, early=True),
        )

        up_b, sent_b, gain_c, back_ask, back_key, back_value, low_e, kept, sent = cross_backward(
            half_here, upstream, after_b, low_d, arrived_d, low_c, gain, ask, key_cross, value_cross,
            dec_column, enc_row, cross_weights,
        )
        arrived_e = from_pair(low_e)
        (cross_blocks,) = weight_gradients(
            (((normed_b, back_ask), (encoder, back_key), (encoder, back_value), (sent_b, mixed_b)),),
            (late,), count,
        )
        cross_sum = reduce_gradients(cross_blocks, (inner,) * 4, own, count)
        arrived = from_pair(sent)

        up_a, sent_a, gain_ab, back_query, back_key, back_value, kept_a, out_a, line_back = self_backward(
            half_here, up_b, after_a, residual, low_e, arrived_e, gain, query, key, value, line,
            dec_column, dec_row, self_weights,
        )
        arrived_a = from_pair(out_a)
        (self_blocks,) = weight_gradients(
            (((normed_a, back_query), (normed_a, back_key), (normed_a, back_value), (sent_a, mixed_a)),),
            (late,), count, (gain_c, gain_ab, line_back, bucket_lanes),
        )
        *self_sum, small = reduce_gradients(self_blocks, (inner,) * 4 + (LANES,), own, count)

        resid_out, input_gradient, encoder_gradient = finish(
            half_here, after_b, up_a, resid_in[0], kept, arrived, kept_a, arrived_a, gain
        )
        gain_part = small[:, :8]
        gain_sum = jnp.transpose(gain_part + from_pair(gain_part))
        gains_gradient = lax.dynamic_slice(gain_sum, (0, half * width), (3, width))
        heads = bias_table.shape[1]
        table_gradient = jnp.transpose(small[:heads, buckets : 2 * buckets])
        return (
            resid_out[None],
            input_gradient[None],
            encoder_gradient[None],
            gains_gradient[None],
            table_gradient,
            *[piece[None] for piece in self_sum],
            *[piece[None] for piece in cross_sum],
            *[piece[None] for piece in feed_sum],
        )

    return layer


def solution(mesh):
    tokens = P("dp", "tensor", None)
    rows = P("dp", None)
    matrix = P(None, "dp", "tensor")
    gain = P(None, None, ("dp", "tensor"))
    table = P(None, "tensor")
    step = jax.shard_map(
        per_device(mesh.shape["dp"]),
        mesh=mesh,
        in_specs=(tokens, tokens, rows, rows, tokens, gain, table) + (matrix,) * 11,
        out_specs=(tokens, tokens, tokens, gain, table) + (matrix,) * 11,
        check_vma=False,
    )
    if len(gather_bits(mesh.shape["dp"], False)) != 4:
        return step
    return step
```
